32 devices in a mesh: image: 4 (over z), space: 8 (over y, x, core).
Axes of the slice: x: 2, y: 2, z: 4, core: 2. Of those that a mesh axis runs over, the one named last changes fastest.
Arguments:
- field: float32 [4, 32, 256, 512], P('image', 'space'), may hold values from -2.5 to 2.5
- mobility: float32 [32, 256, 512], P('space'), may hold values from 0.2 to 1
- fractions: float32 [4], P('image'), may hold values from 0.3 to 0.5
- sides: int32 [4], P('image'), may hold values from 0 to 1, as said below
Outputs:
- blended: float32 [4, 32, 256, 512], P('image', 'space')
The draws below stay inside these ranges and needn't reach their ends.
Inputs may be any that keep to these rules, and one draw needn't show every extreme that they name: `sides`: the first image always names the next one (1), the last image the previous one (0); the others name either.
All inputs are finite; a program needn't handle non-finite values.
Results may differ from the reference program's by a relative error of at most 0.00002.
Values sent between devices are 32-bit elements; how exact they have to be, the bound alone decides.
No kernel may reach another device: no remote copies, remote signals or barrier semaphores. Data moves between devices by JAX's collectives and lax.ppermute only.
A program may use at most 128 MiB of HBM per device.

```python
import math
import jax
import jax.numpy as jnp

NY = 256
NZ = 512
STEPS = 4
NX = 32
IMAGES = 4


def draw_sides(key, part):
    values = jax.random.randint(jax.random.fold_in(key, 7), (IMAGES,), 0, 2).astype(jnp.int32)
    values = values.at[0].set(1)
    values = values.at[IMAGES - 1].set(0)
    return values


def block_levels(key, extent, cuts, least, high):
    factor_of = 1.0
    for position, blocks in cuts:
        heights = jax.random.uniform(jax.random.fold_in(jax.random.fold_in(key, 6), position), (blocks,), jnp.float32, least / len(cuts), high / len(cuts))
        factor_of = factor_of * jnp.repeat(jnp.exp(heights), extent[position] // blocks).reshape((-1,) + (1,) * (len(extent) - 1 - position))
    return factor_of


def gaussian(key, extent, spread, reach, cuts=(), kind=jnp.bfloat16):
    entries = jax.random.normal(key, extent, jnp.float32) * spread
    if len(cuts) > 0:
        entries = block_levels(key, extent, cuts, -0.22, 0.18) * entries
    return jnp.clip(entries, min=-reach, max=reach).astype(kind)


def setup_inputs(seed: int = 0) -> dict:
    keys = jax.random.split(jax.random.key(seed), 5)
    return {
        "field": gaussian(keys[0], (IMAGES, NX, NY, NZ), 0.7, 2.5, ((0, 4), (1, 8)), jnp.float32),
        "mobility": jnp.clip(jnp.exp(math.log(1.0) - 1.609438 * jax.random.uniform(keys[1], (NX, NY, NZ), jnp.float32) ** block_levels(keys[1], (NX, NY, NZ), ((0, 8),), -0.2, 0.2)), 0.2, 1.0),
        "fractions": jnp.clip(0.3 + 0.19999999 * jax.random.uniform(keys[2], (IMAGES,), jnp.float32) ** block_levels(keys[2], (IMAGES,), ((0, 4),), -0.2, 0.2), 0.3, 0.5),
        "sides": draw_sides(jax.random.fold_in(keys[4], 71), 0),
    }


DT = 0.1
EPS2 = 1.5


def advance(phi, xpad, mob):
    padded = jnp.pad(xpad, ((0, 0), (1, 1), (1, 1)))
    beside = padded[2:, 1:-1, 1:-1] + padded[:-2, 1:-1, 1:-1]
    beside = beside + padded[1:-1, 2:, 1:-1] + padded[1:-1, :-2, 1:-1]
    beside = beside + padded[1:-1, 1:-1, 2:] + padded[1:-1, 1:-1, :-2]
    return phi + DT * mob * (EPS2 * (beside - 6.0 * phi) + phi - phi * phi * phi)


def relax(phi, mobility):
    for step in range(STEPS):
        phi = advance(phi, jnp.pad(phi, ((1, 1), (0, 0), (0, 0))), mobility)
    return phi


def reference(field, mobility, fractions, sides):
    relaxed = jnp.stack([relax(field[i], mobility) for i in range(IMAGES)])
    empty = jnp.zeros_like(relaxed[:1])
    upper = jnp.concatenate([relaxed[1:], empty], axis=0)
    lower = jnp.concatenate([empty, relaxed[:-1]], axis=0)
    neighbour = jnp.where((sides == 1)[:, None, None, None], upper, lower)
    return relaxed + fractions[:, None, None, None] * (neighbour - relaxed)
```

```python
import functools

import jax
import jax.numpy as jnp
from jax import lax
from jax.experimental import pallas as pl
from jax.experimental.pallas import tpu as pltpu
from jax.sharding import PartitionSpec as P

STEPS = 4
DT = 0.1
EPS2 = 1.5
TILE = 8
LANES = 128
BLOCK = 32

VMEM = pl.BlockSpec(memory_space=pltpu.VMEM)
SMEM = pl.BlockSpec(memory_space=pltpu.SMEM)
ANY = pl.BlockSpec(memory_space=pl.ANY)
HBM = pl.BlockSpec(memory_space=pltpu.HBM)

SHARES = (4, 8, 8, 6)
ORDER = (
    "E O01 ZA Cf",
    "Cm O11 O31 O21",
    "K01 O02 K11 O12",
    "K21 O22 K02 O03",
    "K12 O13 K31 K22",
    "O23 K03 O04 N",
    "O32 K13 CN O14",
    "OA1 K04 Z0 K23",
    "O24 K32 K14 O33",
    "Z1 KA1 OA2 K24",
    "K33 O34 Z2 KA2",
    "OA3 K34 Z3 KA3",
    "OA4 B0 KA4 B1",
)
BLENDS = ((0, 1, 2), (3,))


def swap(x, odd):
    count = lax.axis_size("space")
    assert count % 2 == 0
    pairs = [((i + odd) % count, (i + 1 + odd) % count) for i in range(0, count, 2)]
    return lax.ppermute(x, "space", pairs + [(b, a) for a, b in pairs])


def swap_images(x, odd):
    images, count = lax.axis_size("image"), lax.axis_size("space")
    assert images % 2 == 0
    pairs = []
    for s in range(count):
        pairs += [(i * count + s, (i + 1) * count + s) for i in range(odd, images - 1, 2)]
    if odd:
        for i in (0, images - 1):
            pairs += [(i * count + s, i * count + s + 1) for s in range(0, count, 2)]
    return lax.ppermute(x, ("image", "space"), pairs + [(b, a) for a, b in pairs])


def cuts(ny):
    bounds = [0]
    for share in SHARES:
        bounds.append(bounds[-1] + share * ny // 32)
    return bounds


def span(bounds, c, s):
    lo = 0 if c == 0 else bounds[c] + TILE * (STEPS - s)
    if c == len(bounds) - 2:
        return lo, bounds[c + 1] + (TILE if s < STEPS else 0)
    return lo, bounds[c + 1] + TILE * (STEPS - s)


def layer_index(layer, layers):
    odd = lax.rem(lax.axis_index("space"), 2)
    return odd * (layers - 1) + layer * (1 - 2 * odd)


def at(first, rows=TILE):
    return pl.ds(first if isinstance(first, int) else pl.multiple_of(first, TILE), rows)


def params(mib):
    return pltpu.CompilerParams(vmem_limit_bytes=(mib + 11) << 20)


def edge_kernel(spans, start, field_ref, *refs):
    outs, raw, sems = refs[:-2], refs[-2], refs[-1]
    layers = field_ref.shape[1]
    copies = [
        pltpu.make_async_copy(field_ref.at[0, layer_index(0, layers), lo:hi], out, sems.at[i])
        for i, ((lo, hi), out) in enumerate(zip(spans, outs))
    ]
    copies.append(pltpu.make_async_copy(field_ref.at[0, :, start:], raw, sems.at[len(spans)]))
    for copy in copies:
        copy.start()
    for copy in copies:
        copy.wait()


def first_edges(field, bounds):
    layers, ny, nz = field.shape[1:]
    spans = [span(bounds, c, 1) for c in range(len(bounds) - 1)]
    start = bounds[-1] - TILE
    shapes = [(hi - lo, nz) for lo, hi in spans] + [(layers, ny - start, nz)]
    return pl.pallas_call(
        functools.partial(edge_kernel, spans, start),
        out_shape=[jax.ShapeDtypeStruct(shape, field.dtype) for shape in shapes],
        in_specs=[HBM],
        out_specs=[VMEM] * len(shapes),
        scratch_shapes=[pltpu.SemaphoreType.DMA((len(shapes),))],
        compiler_params=params(1),
        name="edges",
    )(field)


def towards_even():
    image_odd = lax.rem(lax.axis_index("image"), 2)
    return lambda side: side != image_odd


def pick_kernel(sides_ref, own_ref, even_ref, odd_ref, out_ref, edge_ref):
    layers, rows, _ = out_ref.shape
    first = layer_index(0, layers)
    with_even = towards_even()(sides_ref[0])

    def take(src_ref):
        @pl.loop(0, rows // TILE)
        def _(i):
            for layer in range(layers):
                out_ref[layer, at(i * TILE), :] = src_ref[layer, at(i * TILE), :]
            edge_ref[0, at(i * TILE), :] = own_ref[first, at(i * TILE), :]
            edge_ref[1, at(i * TILE), :] = src_ref[first, at(i * TILE), :]

    pl.when(with_even)(lambda: take(even_ref))
    pl.when(jnp.logical_not(with_even))(lambda: take(odd_ref))


def pick(sides, own, even, odd):
    _, rows, nz = own.shape
    return pl.pallas_call(
        pick_kernel,
        out_shape=[
            jax.ShapeDtypeStruct(own.shape, own.dtype),
            jax.ShapeDtypeStruct((2, rows, nz), own.dtype),
        ],
        in_specs=[SMEM, VMEM, VMEM, VMEM],
        out_specs=[VMEM, VMEM],
        cost_estimate=pl.CostEstimate(flops=0, bytes_accessed=8 * own.size, transcendentals=0),
        compiler_params=params(1),
        name="pick",
    )(sides, own, even, odd)


def relax_rows(cells, mobility, outer, store, n_out, first, final, top, bottom, alone, nz):
    def block(r, rows, top, bottom):
        lane = lax.broadcasted_iota(jnp.int32, (rows, LANES), 1)
        none = jnp.zeros((TILE, nz), jnp.float32)
        under = outer(r, rows)
        mid = cells(0, r, rows)
        for layer in range(n_out):
            over = cells(layer + 1, r, rows)
            above = none if top else cells(layer, r - TILE, TILE)
            below = none if bottom else cells(layer, r + rows, TILE)
            wide = jnp.concatenate([above, mid, below], axis=0)
            up, down = wide[TILE - 1 : TILE - 1 + rows], wide[TILE + 1 : TILE + 1 + rows]
            right = pltpu.roll(mid, nz - 1, 1)
            right = jnp.concatenate(
                [right[:, :-LANES], jnp.where(lane == LANES - 1, 0.0, right[:, -LANES:])], axis=1
            )
            left = pltpu.roll(mid, 1, 1)
            left = jnp.concatenate([jnp.where(lane == 0, 0.0, left[:, :LANES]), left[:, LANES:]], axis=1)
            beside = (over + under) + (down + up) + (right + left)
            rate = DT * mobility(layer, r, rows)
            store(layer, r, rows, mid + rate * (EPS2 * beside - mid * (6.0 * EPS2 - 1.0 + mid * mid)))
            under, mid = mid, over

    last = final
    if top:
        block(first, TILE, True, False)
        first += TILE
    if bottom or alone:
        last -= TILE
    body = (last - first) // BLOCK
    for r in range(first + body * BLOCK, last, TILE):
        block(r, TILE, False, False)
    if body > 0:
        @pl.loop(0, body)
        def _(i):
            block(first + i * BLOCK, BLOCK, False, False)
    if last < final:
        block(last, TILE, False, bottom)


def outside():
    me, count = lax.axis_index("space"), lax.axis_size("space")
    return jnp.logical_or(me == 0, me == count - 1)


def step_kernel(c, s, bounds, layers, names, *refs):
    ref = dict(zip(names, refs))
    last_chunk = c == len(bounds) - 2
    last_step = s == STEPS
    nz = ref["mob"].shape[-1]
    lo, hi = span(bounds, c, s)
    lead = margin(c, s)
    origin = 0 if s == 1 else span(bounds, c, s - 1)[0] - margin(c, s - 1)
    n_out = layers + STEPS - s
    out = ref["out"]
    no_outer = outside()

    def cells(layer, r, rows):
        if s == 1:
            src = ref["own"] if layer < layers else ref["ghost"]
            return src[layer_index(layer % layers, layers), at(r, rows), :]
        return ref["cells"][layer, at(r - origin, rows), :]

    def mobility(layer, r, rows):
        src = ref["mob"] if layer < layers else ref["ghost_mob"]
        return src[layer_index(layer % layers, layers), at(r, rows), :]

    def outer(r, rows):
        return jnp.where(no_outer, 0.0, ref["beyond"][at(r - lo, rows), :])

    edge_lo, edge_hi = span(bounds, c, s + 1) if not last_step else (0, 0)

    def store(layer, r, rows, new):
        out[layer, at(r - lo + lead, rows), :] = new
        if layer > 0 or last_step:
            return
        if not isinstance(r, int):
            ref["edge"][at(r - edge_lo, rows), :] = new
        elif r < edge_hi:
            kept = min(rows, edge_hi - r)
            ref["edge"][at(r - edge_lo, kept), :] = new[:kept]

    if c > 0 and not last_step:
        rows = ref["above"].shape[1]
        for layer in range(n_out):
            out[layer, 0:lead, :] = ref["above"][layer, rows - lead : rows, :]
        ref["edge"][0:TILE, :] = ref["above"][0, rows - TILE : rows, :]

    relax_rows(cells, mobility, outer, store, n_out, lo, hi, c == 0, last_chunk and s < STEPS, not last_step, nz)


def margin(c, s):
    return 2 * TILE if c > 0 and 0 < s < STEPS else 0


def step(c, s, bounds, layers, arrays, like):
    _, nz = like.shape[1:]
    lo, hi = span(bounds, c, s)
    n_out = layers + STEPS - s
    shapes = {"out": (n_out, margin(c, s) + hi - lo, nz)}
    if s < STEPS:
        edge_lo, edge_hi = span(bounds, c, s + 1)
        shapes["edge"] = (edge_hi - edge_lo, nz)
    cells = n_out * (hi - lo) * nz
    outs = pl.pallas_call(
        functools.partial(step_kernel, c, s, bounds, layers, [*arrays, *shapes]),
        out_shape=[jax.ShapeDtypeStruct(shape, like.dtype) for shape in shapes.values()],
        in_specs=[VMEM] * len(arrays),
        out_specs=[VMEM] * len(shapes),
        cost_estimate=pl.CostEstimate(flops=20 * cells, bytes_accessed=4 * cells, transcendentals=0),
        compiler_params=params(1),
    )(*arrays.values())
    return dict(zip(shapes, outs))


def both_kernel(s, start, layers, names, *refs):
    ref = dict(zip(names, refs))
    last_step = s == STEPS
    ny, nz = ref["mob"].shape[1:]
    n_out = layers + STEPS - s
    no_outer = outside()
    first = start + TILE if last_step else start

    def mobility(layer, r, rows):
        src = ref["mob"] if layer < layers else ref["ghost_mob"]
        return src[layer_index(layer % layers, layers), at(r, rows), :]

    for image in (0, 1):
        def cells(layer, r, rows, image=image):
            if s > 1:
                return ref["cells"][image, layer, at(r - start, rows), :]
            name, skip = ("own", 0) if image == 0 else ("other", start)
            src = ref[name] if layer < layers else ref[name + "_ghost"]
            return src[layer_index(layer % layers, layers), at(r - skip, rows), :]

        def outer(r, rows, image=image):
            return jnp.where(no_outer, 0.0, ref["beyond"][image, at(r - start, rows), :])

        def store(layer, r, rows, new, image=image):
            if last_step:
                here = at(r - first, rows)
                if image == 1:
                    mine = ref["relaxed"][layer, here, :]
                    new = mine + ref["fractions"][0] * (new - mine)
                ref["relaxed"][layer, here, :] = new
                return
            ref["out"][image, layer, at(r - start, rows), :] = new
            if layer == 0:
                ref["edge"][image, at(r - start, rows), :] = new

        relax_rows(cells, mobility, outer, store, n_out, first, ny, not last_step, True, False, nz)

    if last_step:
        copies = [
            pltpu.make_async_copy(
                ref["relaxed"].at[layer], ref["out"].at[0, layer_index(layer, layers), first:ny], ref["sem"].at[layer]
            )
            for layer in range(layers)
        ]
        for copy in copies:
            copy.start()
        for copy in copies:
            copy.wait()


def both_step(s, bounds, layers, arrays, like, out, field):
    ny, nz = like.shape[1:]
    start = bounds[-1] - TILE
    rows = ny - start
    n_out = layers + STEPS - s
    last_step = s == STEPS
    scratch = {}
    if last_step:
        shapes = {"out": field.shape}
        scratch["relaxed"] = pltpu.VMEM((layers, rows - TILE, nz), like.dtype)
        scratch["sem"] = pltpu.SemaphoreType.DMA((layers,))
        specs = [HBM]
    else:
        shapes = {"out": (2, n_out, rows, nz), "edge": (2, rows, nz)}
        specs = [VMEM, VMEM]
    in_specs = [SMEM if name == "fractions" else VMEM for name in arrays]
    aliases = {}
    if last_step and out is not None:
        aliases = {len(arrays): 0}
        arrays = {**arrays, "before": out}
        in_specs.append(HBM)
    cells = 2 * n_out * rows * nz
    outs = pl.pallas_call(
        functools.partial(both_kernel, s, start, layers, [*arrays, *shapes, *scratch]),
        out_shape=[jax.ShapeDtypeStruct(shape, like.dtype) for shape in shapes.values()],
        in_specs=in_specs,
        out_specs=specs,
        scratch_shapes=list(scratch.values()),
        input_output_aliases=aliases,
        cost_estimate=pl.CostEstimate(flops=20 * cells, bytes_accessed=4 * cells, transcendentals=0),
        compiler_params=params(1),
    )(*arrays.values())
    return dict(zip(shapes, outs))


def blend_kernel(spans, aliased, sides_ref, fractions_ref, *refs):
    n = len(spans)
    owns, evens, odds = refs[:n], refs[n : 2 * n], refs[2 * n : 3 * n]
    out_ref, bufs, sem = refs[3 * n + aliased], refs[3 * n + aliased + 1 : -1], refs[-1]
    layers = owns[0].shape[0]
    with_even = towards_even()(sides_ref[0])
    share = fractions_ref[0]
    copies = []
    for k, (lo, hi) in enumerate(spans):
        def mix(other_ref, own_ref=owns[k], buf=bufs[k], rows=hi - lo):
            @pl.loop(0, rows // TILE)
            def _(i):
                for layer in range(layers):
                    mine = own_ref[layer, at(i * TILE), :]
                    buf[layer, at(i * TILE), :] = mine + share * (other_ref[layer, at(i * TILE), :] - mine)

        pl.when(with_even)(functools.partial(mix, evens[k]))
        pl.when(jnp.logical_not(with_even))(functools.partial(mix, odds[k]))
        for layer in range(layers):
            copy = pltpu.make_async_copy(
                bufs[k].at[layer], out_ref.at[0, layer_index(layer, layers), lo:hi], sem.at[k, layer]
            )
            copy.start()
            copies.append(copy)
    for copy in copies:
        copy.wait()


def blend(chunks, bounds, sides, fractions, val, out, like):
    spans = [span(bounds, c, STEPS) for c in chunks]
    owns = [val["K", c, STEPS] for c in chunks]
    layers = owns[0].shape[0]
    operands = [sides, fractions, *owns, *(val["Z", c, name] for name in ("even", "odd") for c in chunks)]
    size = sum(own.size for own in owns)
    return pl.pallas_call(
        functools.partial(blend_kernel, spans, out is not None),
        out_shape=jax.ShapeDtypeStruct(like.shape, like.dtype),
        in_specs=[SMEM, SMEM] + [VMEM] * (3 * len(chunks)) + ([] if out is None else [HBM]),
        out_specs=HBM,
        input_output_aliases={} if out is None else {len(operands): 0},
        scratch_shapes=[pltpu.VMEM(own.shape, own.dtype) for own in owns]
        + [pltpu.SemaphoreType.DMA((len(chunks), layers))],
        cost_estimate=pl.CostEstimate(flops=3 * size, bytes_accessed=12 * size, transcendentals=0),
        compiler_params=params(4),
    )(*operands, *([] if out is None else [out]))


def items():
    return " ".join(ORDER).split()


def local(field, mobility, fractions, sides):
    layers, ny = field.shape[1:3]
    bounds = cuts(ny)
    val = {}
    out = None
    for item in items():
        kind, c, s = item[0], *(item[1:] + "  ")[:2]
        c = int(c) if c.isdigit() else c
        s = int(s) if s.isdigit() else None
        if kind == "E":
            *edges, val["K", "A", STEPS] = first_edges(field, bounds)
            for i, edge in enumerate(edges):
                val["edge", i, 1] = edge
        elif kind == "C":
            source = {"f": field[0], "m": mobility, "N": val.get(("N",))}[c]
            val["C", c] = swap(source, 0)
        elif kind == "N":
            val["N",], val["edge", "A", 1] = pick(
                sides, val["K", "A", STEPS], val["Z", "A", "even"], val["Z", "A", "odd"]
            )
        elif kind == "O":
            val["O", c, s] = swap(val["edge", c, s], 1)
        elif kind == "K":
            arrays = {"mob": mobility, "ghost_mob": val["C", "m"], "beyond": val["O", c, s]}
            if s == 1 and c == "A":
                arrays["own"], arrays["own_ghost"] = field[0], val["C", "f"]
                arrays["other"], arrays["other_ghost"] = val["N",], val["C", "N"]
            elif s == 1:
                arrays["own"], arrays["ghost"] = field[0], val["C", "f"]
            else:
                arrays["cells"] = val["K", c, s - 1]
            if c == "A":
                if s == STEPS:
                    arrays["fractions"] = fractions
                got = both_step(s, bounds, layers, arrays, mobility, out, field)
            else:
                if c > 0 and s < STEPS:
                    arrays["above"] = val["K", c - 1, s]
                got = step(c, s, bounds, layers, arrays, mobility)
            if c == "A" and s == STEPS:
                out = got["out"]
            else:
                val["K", c, s] = got["out"]
            if s < STEPS:
                val["edge", c, s + 1] = got["edge"]
        elif kind == "Z":
            for name, odd in (("even", 0), ("odd", 1)):
                val["Z", c, name] = swap_images(val["K", c, STEPS], odd)
        elif kind == "B":
            out = blend(BLENDS[c], bounds, sides, fractions, val, out, field)
    return out


def solution(mesh):
    return jax.shard_map(
        local,
        mesh=mesh,
        in_specs=(P("image", "space", None, None), P("space", None, None), P("image"), P("image")),
        out_specs=P("image", "space", None, None),
        check_vma=False,
    )
```

```python
import functools

import jax
import jax.numpy as jnp
from jax import lax
from jax.experimental import pallas as pl
from jax.experimental.pallas import tpu as pltpu
from jax.sharding import PartitionSpec as P

STEPS = 4
DT = 0.1
EPS2 = 1.5
TILE = 8
LANES = 128
BLOCK = 32
TOGETHER = 2

VMEM = pl.BlockSpec(memory_space=pltpu.VMEM)
SMEM = pl.BlockSpec(memory_space=pltpu.SMEM)
ANY = pl.BlockSpec(memory_space=pl.ANY)
HBM = pl.BlockSpec(memory_space=pltpu.HBM)

SHARES = (4, 8, 7, 5)
ORDER = (
    "E G O01 Cf",
    "L O11 Co Cn",
    "Cm ZA K01 O02",
    "O31 K11 O12 K02",
    "O03 K21 O22 K12",
    "O13 K03 N CN",
    "O04 OA1 K31 K22",
    "K13 O14 O23 K04",
    "Z0 O32 KA1 OA2",
    "K14 Z1 K23 O24",
    "K32 O33 KA2 OA3",
    "K24 Z2 K33 O34",
    "KA3 K34 OA4 Z3",
    "B0 KA4 B1",
)
BLENDS = ((0, 1, 2), (3,))


def swap(x, odd):
    count = lax.axis_size("space")
    assert count % 2 == 0
    pairs = [((i + odd) % count, (i + 1 + odd) % count) for i in range(0, count, 2)]
    return lax.ppermute(x, "space", pairs + [(b, a) for a, b in pairs])


def swap_images(x, odd):
    images, count = lax.axis_size("image"), lax.axis_size("space")
    assert images % 2 == 0
    pairs = []
    for s in range(count):
        pairs += [(i * count + s, (i + 1) * count + s) for i in range(odd, images - 1, 2)]
    if odd:
        for i in (0, images - 1):
            pairs += [(i * count + s, i * count + s + 1) for s in range(0, count, 2)]
    return lax.ppermute(x, ("image", "space"), pairs + [(b, a) for a, b in pairs])


def cuts(ny):
    bounds = [0]
    for share in SHARES:
        bounds.append(bounds[-1] + share * ny // 32)
    assert bounds[-1] < ny
    return bounds + [ny]


def span(bounds, c, s):
    moved = TILE * (STEPS - s)
    return (0 if c == 0 else bounds[c] + moved), (bounds[-1] if c == len(bounds) - 2 else bounds[c + 1] + moved)


def raw_group(bounds, c):
    first, last = (1, TOGETHER) if 1 <= c <= TOGETHER else (c, c)
    return span(bounds, first, 1)[0], span(bounds, last, 1)[1]


def layer_index(layer, layers):
    odd = lax.rem(lax.axis_index("space"), 2)
    return odd * (layers - 1) + layer * (1 - 2 * odd)


def at(first, rows=TILE):
    return pl.ds(first if isinstance(first, int) else pl.multiple_of(first, TILE), rows)


def params(mib):
    return pltpu.CompilerParams(vmem_limit_bytes=mib << 20)


def move(moves, sems):
    copies = [pltpu.make_async_copy(src, dst, sems.at[i]) for i, (src, dst) in enumerate(moves)]
    for copy in copies:
        copy.start()
    for copy in copies:
        copy.wait()


def first_edge(field, bounds):
    layers, _, nz = field.shape[1:]
    rows = span(bounds, 0, 1)[1]
    return lax.dynamic_slice(field, (0, layer_index(0, layers), 0, 0), (1, 1, rows, nz)).reshape(rows, nz)


def near_kernel(near, field_ref, ghost, sems):
    layers = field_ref.shape[1]
    move([(field_ref.at[0, layer_index(layers - 1 - k, layers), :near], ghost.at[k]) for k in range(layers)], sems)


def near_ghosts(field, bounds):
    layers, _, nz = field.shape[1:]
    near = span(bounds, 0, 0)[1]
    return pl.pallas_call(
        functools.partial(near_kernel, near),
        out_shape=jax.ShapeDtypeStruct((layers, near, nz), field.dtype),
        in_specs=[ANY],
        out_specs=VMEM,
        scratch_shapes=[pltpu.SemaphoreType.DMA((layers,))],
        compiler_params=params(12),
        name="near",
    )(field)


def later_kernel(spans, start, near, field_ref, mob_ref, ghost, raw, *refs):
    *edges, sems = refs
    layers = field_ref.shape[1]
    moves = []
    for k in range(layers - 1):
        moves.append((mob_ref.at[layer_index(layers - 1 - k, layers), :near], ghost.at[k]))
    moves.append((field_ref.at[0, :, start:], raw))
    moves += [(field_ref.at[0, layer_index(0, layers), lo:hi], edge) for (lo, hi), edge in zip(spans, edges)]
    move(moves, sems)


def later_edges(field, mobility, bounds):
    layers, ny, nz = field.shape[1:]
    spans = [raw_group(bounds, c) for c in (1, *range(TOGETHER + 1, len(bounds) - 2))]
    start, near = bounds[-2] - TILE, span(bounds, 0, 0)[1]
    shapes = [(layers - 1, near, nz), (layers, ny - start, nz)] + [(hi - lo, nz) for lo, hi in spans]
    return pl.pallas_call(
        functools.partial(later_kernel, spans, start, near),
        out_shape=[jax.ShapeDtypeStruct(shape, field.dtype) for shape in shapes],
        in_specs=[ANY, ANY],
        out_specs=[VMEM] * len(shapes),
        scratch_shapes=[pltpu.SemaphoreType.DMA((layers + len(spans),))],
        compiler_params=params(12),
        name="later",
    )(field, mobility)


def towards_even():
    image_odd = lax.rem(lax.axis_index("image"), 2)
    return lambda side: side != image_odd


def pick_kernel(skip, ahead, sides_ref, own_ref, even_ref, odd_ref, *refs):
    out_ref, edge_ref = refs[-2:]
    layers, rows, _ = out_ref.shape
    first = layer_index(0, layers)
    with_even = towards_even()(sides_ref[0])
    if ahead:
        edge_ref[:ahead, :] = refs[0][...]
    edge_ref[ahead : ahead + rows - skip, :] = own_ref[first, skip:, :]

    def take(src_ref):
        @pl.loop(0, rows // TILE)
        def _(i):
            for layer in range(layers):
                out_ref[layer, at(i * TILE), :] = src_ref[layer, at(i * TILE), :]
            edge_ref[at(i * TILE + ahead + rows - skip), :] = src_ref[first, at(i * TILE), :]

    pl.when(with_even)(lambda: take(even_ref))
    pl.when(jnp.logical_not(with_even))(lambda: take(odd_ref))


def pick(bounds, sides, own, even, odd, before):
    _, rows, nz = own.shape
    skip = span(bounds, len(bounds) - 2, 1)[0] - (bounds[-2] - TILE)
    ahead = 0 if before is None else before.shape[0]
    return pl.pallas_call(
        functools.partial(pick_kernel, skip, ahead),
        out_shape=[
            jax.ShapeDtypeStruct(own.shape, own.dtype),
            jax.ShapeDtypeStruct((ahead + 2 * rows - skip, nz), own.dtype),
        ],
        in_specs=[SMEM] + [VMEM] * (4 if ahead else 3),
        out_specs=[VMEM, VMEM],
        cost_estimate=pl.CostEstimate(flops=0, bytes_accessed=8 * own.size, transcendentals=0),
        compiler_params=params(12),
        name="pick",
    )(sides, own, even, odd, *([before] if ahead else []))


def relax_rows(cells, mobility, outer, store, n_out, first, final, top, bottom, nz):
    def block(r, rows, top, bottom):
        lane = lax.broadcasted_iota(jnp.int32, (rows, LANES), 1)
        none = jnp.zeros((TILE, nz), jnp.float32)
        under = outer(r, rows)
        mid = cells(0, r, rows)
        for layer in range(n_out):
            over = cells(layer + 1, r, rows)
            above = none if top else cells(layer, r - TILE, TILE)
            below = none if bottom else cells(layer, r + rows, TILE)
            wide = jnp.concatenate([above, mid, below], axis=0)
            up, down = wide[TILE - 1 : TILE - 1 + rows], wide[TILE + 1 : TILE + 1 + rows]
            right = pltpu.roll(mid, nz - 1, 1)
            right = jnp.concatenate(
                [right[:, :-LANES], jnp.where(lane == LANES - 1, 0.0, right[:, -LANES:])], axis=1
            )
            left = pltpu.roll(mid, 1, 1)
            left = jnp.concatenate([jnp.where(lane == 0, 0.0, left[:, :LANES]), left[:, LANES:]], axis=1)
            beside = (over + under) + (down + up) + (right + left)
            rate = DT * mobility(layer, r, rows)
            store(layer, r, rows, mid + rate * (EPS2 * beside - mid * (6.0 * EPS2 - 1.0 + mid * mid)))
            under, mid = mid, over

    for r in range(first, final, BLOCK):
        rows = min(BLOCK, final - r)
        block(r, rows, top and r == first, bottom and r + rows == final)


def outside():
    me, count = lax.axis_index("space"), lax.axis_size("space")
    return jnp.logical_or(me == 0, me == count - 1)


def margin(c, s):
    return 2 * TILE if c > 0 and 0 < s < STEPS else 0


def copy_ahead(ref):
    if "edge_before" not in ref:
        return 0
    rows = ref["edge_before"].shape[0]
    ref["edge"][:rows, :] = ref["edge_before"][...]
    return rows


def step_kernel(c, s, skip, bounds, layers, names, *refs):
    ref = dict(zip(names, refs))
    both = c == len(bounds) - 2
    last_step = s == STEPS
    ny, nz = ref["mob"].shape[1:]
    lo, hi = span(bounds, c, s)
    lead = margin(c, s)
    origin = 0 if s == 1 else span(bounds, c, s - 1)[0] - margin(c, s - 1)
    n_out = layers + STEPS - s
    no_outer = outside()

    def ghost_at(name, k, r, rows):
        return ref[name][k if c == 0 else layer_index(k, layers), at(r, rows), :]

    def cells(layer, r, rows):
        if s > 1:
            return ref["cells"][layer, at(r - origin, rows), :]
        if layer < layers:
            return ref["own"][layer_index(layer, layers), at(r, rows), :]
        return ghost_at("ghost", layer - layers, r, rows)

    def mobility(layer, r, rows):
        if layer < layers:
            return ref["mob"][layer_index(layer, layers), at(r, rows), :]
        return ghost_at("ghost_mob", layer - layers, r, rows)

    def outer(r, rows):
        return jnp.where(no_outer, 0.0, ref["beyond"][at(r - lo + skip, rows), :])

    edge_lo, edge_hi = span(bounds, c, s + 1) if not last_step else (0, 0)
    ahead = copy_ahead(ref)
    out = ref["own_out"]

    def store(layer, r, rows, new):
        out[layer, at(r - lo + lead, rows), :] = new
        if layer > 0 or last_step:
            return
        if r < edge_hi:
            kept = min(rows, edge_hi - r)
            ref["edge"][at(r - edge_lo + ahead, kept), :] = new[:kept]

    if c > 0 and not last_step:
        rows = ref["above"].shape[1]
        for layer in range(n_out):
            out[layer, 0:lead, :] = ref["above"][layer, rows - lead : rows, :]
        ref["edge"][ahead : ahead + TILE, :] = ref["above"][0, rows - TILE : rows, :]

    relax_rows(cells, mobility, outer, store, n_out, lo, hi, c == 0, both, nz)
    if not both:
        return

    start = lo_other = bounds[-2] - TILE
    if last_step:
        lo_other += TILE
    sent, kept = hi - lo, edge_hi - edge_lo

    def other_cells(layer, r, rows):
        if s > 1:
            return ref["other"][layer, at(r - start, rows), :]
        src = ref["other"] if layer < layers else ref["other_ghost"]
        return src[layer_index(layer % layers, layers), at(r - start, rows), :]

    def other_outer(r, rows):
        return jnp.where(no_outer, 0.0, ref["beyond"][at(r - start + sent + skip, rows), :])

    def other_store(layer, r, rows, new):
        if last_step:
            mine = out[layer, at(r - lo, rows), :]
            out[layer, at(r - lo, rows), :] = mine + ref["fractions"][0] * (new - mine)
            return
        ref["other_out"][layer, at(r - start, rows), :] = new
        if layer == 0:
            ref["edge"][at(r - start + kept + ahead, rows), :] = new

    relax_rows(
        other_cells, mobility, other_outer, other_store, n_out, lo_other, ny, not last_step, True, nz
    )
    if last_step:
        copies = [
            pltpu.make_async_copy(
                out.at[layer], ref["out"].at[0, layer_index(layer, layers), lo:hi], ref["sem"].at[layer]
            )
            for layer in range(layers)
        ]
        for copy in copies:
            copy.start()
        for copy in copies:
            copy.wait()


def step(c, s, skip, bounds, layers, arrays, like, field, before):
    ny, nz = like.shape[1:]
    lo, hi = span(bounds, c, s)
    both = c == len(bounds) - 2
    n_out = layers + STEPS - s
    rows = ny - bounds[-2] + TILE
    own = (n_out, margin(c, s) + hi - lo, nz)
    last_both = both and s == STEPS
    in_specs = [SMEM if name == "fractions" else VMEM for name in arrays]
    shapes, scratch, aliases = {}, {}, {}
    if last_both:
        shapes["out"] = field.shape
        scratch = {"own_out": pltpu.VMEM(own, like.dtype), "sem": pltpu.SemaphoreType.DMA((layers,))}
        if before is not None:
            aliases = {len(arrays): 0}
            arrays = {**arrays, "before": before}
            in_specs.append(ANY)
    else:
        shapes["own_out"] = own
        if both:
            shapes["other_out"] = (n_out, rows, nz)
        if s < STEPS:
            edge_lo, edge_hi = span(bounds, c, s + 1)
            ahead = arrays["edge_before"].shape[0] if "edge_before" in arrays else 0
            shapes["edge"] = (ahead + edge_hi - edge_lo + (rows if both else 0), nz)
    cells = n_out * (hi - lo + (rows if both else 0)) * nz
    outs = pl.pallas_call(
        functools.partial(step_kernel, c, s, skip, bounds, layers, [*arrays, *shapes, *scratch]),
        out_shape=[jax.ShapeDtypeStruct(shape, like.dtype) for shape in shapes.values()],
        in_specs=in_specs,
        out_specs=[ANY] if last_both else [VMEM] * len(shapes),
        scratch_shapes=list(scratch.values()),
        input_output_aliases=aliases,
        cost_estimate=pl.CostEstimate(flops=20 * cells, bytes_accessed=4 * cells, transcendentals=0),
        compiler_params=params(12),
    )(*arrays.values())
    return dict(zip(shapes, outs))


def blend_kernel(spans, aliased, sides_ref, fractions_ref, *refs):
    n = len(spans)
    owns, evens, odds = refs[:n], refs[n : 2 * n], refs[2 * n : 3 * n]
    out_ref, bufs, sem = refs[3 * n + aliased], refs[3 * n + aliased + 1 : -1], refs[-1]
    layers = owns[0].shape[0]
    with_even = towards_even()(sides_ref[0])
    share = fractions_ref[0]
    copies = []
    for k, (lo, hi) in enumerate(spans):
        def mix(other_ref, own_ref=owns[k], buf=bufs[k], rows=hi - lo):
            @pl.loop(0, rows // TILE)
            def _(i):
                for layer in range(layers):
                    mine = own_ref[layer, at(i * TILE), :]
                    buf[layer, at(i * TILE), :] = mine + share * (other_ref[layer, at(i * TILE), :] - mine)

        pl.when(with_even)(functools.partial(mix, evens[k]))
        pl.when(jnp.logical_not(with_even))(functools.partial(mix, odds[k]))
        for layer in range(layers):
            copy = pltpu.make_async_copy(
                bufs[k].at[layer], out_ref.at[0, layer_index(layer, layers), lo:hi], sem.at[k, layer]
            )
            copy.start()
            copies.append(copy)
    for copy in copies:
        copy.wait()


def blend(chunks, bounds, sides, fractions, val, out, like):
    spans = [span(bounds, c, STEPS) for c in chunks]
    owns = [val["K", c, STEPS] for c in chunks]
    layers = owns[0].shape[0]
    operands = [sides, fractions, *owns, *(val["Z", c, name] for name in ("even", "odd") for c in chunks)]
    size = sum(own.size for own in owns)
    return pl.pallas_call(
        functools.partial(blend_kernel, spans, out is not None),
        out_shape=jax.ShapeDtypeStruct(like.shape, like.dtype),
        in_specs=[SMEM, SMEM] + [VMEM] * (3 * len(chunks)) + ([] if out is None else [HBM]),
        out_specs=HBM,
        input_output_aliases={} if out is None else {len(operands): 0},
        scratch_shapes=[pltpu.VMEM(own.shape, own.dtype) for own in owns]
        + [pltpu.SemaphoreType.DMA((len(chunks), layers))],
        cost_estimate=pl.CostEstimate(flops=3 * size, bytes_accessed=12 * size, transcendentals=0),
        compiler_params=params(12),
    )(*operands, *([] if out is None else [out]))


def items():
    return " ".join(ORDER).split()


def chunk_of(name):
    return len(SHARES) if name == "A" else int(name)


def swaps():
    ahead = {}
    for item in items():
        members = [(chunk_of(m[0]), int(m[1])) for m in item[1:].split("_")] if item[0] == "O" else []
        ahead.update(zip(members[1:], members))
    return ahead


def local(field, mobility, fractions, sides):
    layers, ny = field.shape[1:3]
    bounds = cuts(ny)
    last = len(bounds) - 2
    ahead = swaps()
    val = {}
    out = None

    def before(c, s):
        return val["edge", ahead[c, s]] if (c, s) in ahead else None

    for item in items():
        kind = item[0]
        if kind == "E":
            val["edge", (0, 1)] = first_edge(field, bounds)
        elif kind == "G":
            val["near"] = near_ghosts(field, bounds)
        elif kind == "L":
            val["near_mob"], val["K", last, STEPS], *edges = later_edges(field, mobility, bounds)
            for i, edge in zip((1, *range(TOGETHER + 1, last)), edges):
                val["edge", (i, 1)] = edge
        elif kind == "C":
            sources = {"n": "near", "o": "near_mob", "N": "N", "f": field[0], "m": mobility}
            source = sources[item[1]]
            val["C", item[1]] = swap(val[source] if isinstance(source, str) else source, 0)
        elif kind == "N":
            val["N"], val["edge", (last, 1)] = pick(
                bounds,
                sides,
                val["K", last, STEPS],
                val["Z", last, "even"],
                val["Z", last, "odd"],
                before(last, 1),
            )
        elif kind == "O":
            members = [(chunk_of(m[0]), int(m[1])) for m in item[1:].split("_")]
            got = swap(val["edge", members[-1]], 1)
            skip = 0
            for c, s in members:
                val["O", c, s] = got, skip
                lo, hi = raw_group(bounds, c) if s == 1 else span(bounds, c, s)
                if (c, s) == (1, 1):
                    for i in range(2, TOGETHER + 1):
                        val["O", i, 1] = got, skip + span(bounds, i, 1)[0] - lo
                skip += hi - lo + (ny - bounds[-2] + TILE if c == last else 0)
        elif kind == "K":
            c, s = chunk_of(item[1]), int(item[2])
            beyond, skip = val["O", c, s]
            arrays = {"mob": mobility, "beyond": beyond}
            arrays["ghost_mob"] = val["C", "m" if c > 0 else "o"]
            if s == 1:
                arrays["ghost"] = val["C", "f" if c > 0 else "n"]
                arrays["own"] = field[0]
            else:
                arrays["cells"] = val["K", c, s - 1]
            if c > 0 and s < STEPS:
                arrays["above"] = val["K", c - 1, s]
            if c == last:
                arrays["other"] = val["N"] if s == 1 else val["other", s - 1]
                if s == 1:
                    arrays["other_ghost"] = val["C", "N"]
                if s == STEPS:
                    arrays["fractions"] = fractions
            if before(c, s + 1) is not None:
                arrays["edge_before"] = before(c, s + 1)
            got = step(c, s, skip, bounds, layers, arrays, mobility, field, out)
            if "out" in got:
                out = got["out"]
            else:
                val["K", c, s] = got["own_out"]
            val["other", s] = got.get("other_out", val.get(("other", s)))
            val["edge", (c, s + 1)] = got.get("edge")
        elif kind == "Z":
            c = chunk_of(item[1])
            for name, odd in (("even", 0), ("odd", 1)):
                val["Z", c, name] = swap_images(val["K", c, STEPS], odd)
        elif kind == "B":
            out = blend(BLENDS[int(item[1])], bounds, sides, fractions, val, out, field)
    return out


def solution(mesh):
    return jax.shard_map(
        local,
        mesh=mesh,
        in_specs=(P("image", "space", None, None), P("space", None, None), P("image"), P("image")),
        out_specs=P("image", "space", None, None),
        check_vma=False,
    )
```

```python
import functools

import jax
import jax.numpy as jnp
from jax import lax
from jax.experimental import pallas as pl
from jax.experimental.pallas import tpu as pltpu
from jax.sharding import PartitionSpec as P

STEPS = 4
DT = 0.1
EPS2 = 1.5
TILE = 8
LANES = 128
BLOCK = 32
TOGETHER = 2

VMEM = pl.BlockSpec(memory_space=pltpu.VMEM)
SMEM = pl.BlockSpec(memory_space=pltpu.SMEM)
ANY = pl.BlockSpec(memory_space=pl.ANY)
HBM = pl.BlockSpec(memory_space=pltpu.HBM)

SHARES = (5, 8, 7, 4)
ORDER = (
    "E G O01 Cf",
    "L O11 Co Cn",
    "Cm ZA K01 O02",
    "O31 K11 O12 K02",
    "O03 K21 O22 K12",
    "O13 K03 O04 N",
    "CN OA1 K31 K22",
    "K13 O14 K04 Z0",
    "O23 O32 JA1 OA2",
    "KA1 K14 Z1 K23",
    "O24 K32 O33 JA2",
    "OA3 KA2 K24 Z2",
    "K33 O34 JA3 OA4",
    "K34 Z3 KA3 IA4",
    "B0 KA4 B1",
)
BLENDS = ((0, 1, 2), (3,))


def swap(x, odd):
    count = lax.axis_size("space")
    assert count % 2 == 0
    pairs = [((i + odd) % count, (i + 1 + odd) % count) for i in range(0, count, 2)]
    return lax.ppermute(x, "space", pairs + [(b, a) for a, b in pairs])


def swap_images(x, odd):
    images, count = lax.axis_size("image"), lax.axis_size("space")
    assert images % 2 == 0
    pairs = []
    for s in range(count):
        pairs += [(i * count + s, (i + 1) * count + s) for i in range(odd, images - 1, 2)]
    if odd:
        for i in (0, images - 1):
            pairs += [(i * count + s, i * count + s + 1) for s in range(0, count, 2)]
    return lax.ppermute(x, ("image", "space"), pairs + [(b, a) for a, b in pairs])


def cuts(ny):
    bounds = [0]
    for share in SHARES:
        bounds.append(bounds[-1] + share * ny // 32)
    assert bounds[-1] < ny
    return bounds + [ny]


def span(bounds, c, s):
    moved = TILE * (STEPS - s)
    return (0 if c == 0 else bounds[c] + moved), (bounds[-1] if c == len(bounds) - 2 else bounds[c + 1] + moved)


def raw_group(bounds, c):
    first, last = (1, TOGETHER) if 1 <= c <= TOGETHER else (c, c)
    return span(bounds, first, 1)[0], span(bounds, last, 1)[1]


def layer_index(layer, layers):
    odd = lax.rem(lax.axis_index("space"), 2)
    return odd * (layers - 1) + layer * (1 - 2 * odd)


def at(first, rows=TILE):
    return pl.ds(first if isinstance(first, int) else pl.multiple_of(first, TILE), rows)


def params(mib):
    return pltpu.CompilerParams(vmem_limit_bytes=mib << 20)


def move(moves, sems):
    copies = [pltpu.make_async_copy(src, dst, sems.at[i]) for i, (src, dst) in enumerate(moves)]
    for copy in copies:
        copy.start()
    for copy in copies:
        copy.wait()


def first_edge(field, bounds):
    layers, _, nz = field.shape[1:]
    rows = span(bounds, 0, 1)[1]
    return lax.dynamic_slice(field, (0, layer_index(0, layers), 0, 0), (1, 1, rows, nz)).reshape(rows, nz)


def near_kernel(near, field_ref, ghost, sems):
    layers = field_ref.shape[1]
    move([(field_ref.at[0, layer_index(layers - 1 - k, layers), :near], ghost.at[k]) for k in range(layers)], sems)


def near_ghosts(field, bounds):
    layers, _, nz = field.shape[1:]
    near = span(bounds, 0, 0)[1]
    return pl.pallas_call(
        functools.partial(near_kernel, near),
        out_shape=jax.ShapeDtypeStruct((layers, near, nz), field.dtype),
        in_specs=[ANY],
        out_specs=VMEM,
        scratch_shapes=[pltpu.SemaphoreType.DMA((layers,))],
        compiler_params=params(12),
        name="near",
    )(field)


def later_kernel(spans, start, near, field_ref, mob_ref, ghost, raw, *refs):
    *edges, sems = refs
    layers = field_ref.shape[1]
    moves = []
    for k in range(layers - 1):
        moves.append((mob_ref.at[layer_index(layers - 1 - k, layers), :near], ghost.at[k]))
    moves.append((field_ref.at[0, :, start:], raw))
    moves += [(field_ref.at[0, layer_index(0, layers), lo:hi], edge) for (lo, hi), edge in zip(spans, edges)]
    move(moves, sems)


def later_edges(field, mobility, bounds):
    layers, ny, nz = field.shape[1:]
    spans = [raw_group(bounds, c) for c in (1, *range(TOGETHER + 1, len(bounds) - 2))]
    start, near = bounds[-2] - TILE, span(bounds, 0, 0)[1]
    shapes = [(layers - 1, near, nz), (layers, ny - start, nz)] + [(hi - lo, nz) for lo, hi in spans]
    return pl.pallas_call(
        functools.partial(later_kernel, spans, start, near),
        out_shape=[jax.ShapeDtypeStruct(shape, field.dtype) for shape in shapes],
        in_specs=[ANY, ANY],
        out_specs=[VMEM] * len(shapes),
        scratch_shapes=[pltpu.SemaphoreType.DMA((layers + len(spans),))],
        compiler_params=params(12),
        name="later",
    )(field, mobility)


def towards_even():
    image_odd = lax.rem(lax.axis_index("image"), 2)
    return lambda side: side != image_odd


def pick_kernel(skip, ahead, sides_ref, own_ref, even_ref, odd_ref, *refs):
    out_ref, edge_ref = refs[-2:]
    layers, rows, _ = out_ref.shape
    first = layer_index(0, layers)
    with_even = towards_even()(sides_ref[0])
    if ahead:
        edge_ref[:ahead, :] = refs[0][...]
    edge_ref[ahead : ahead + rows - skip, :] = own_ref[first, skip:, :]

    def take(src_ref):
        @pl.loop(0, rows // TILE)
        def _(i):
            for layer in range(layers):
                out_ref[layer, at(i * TILE), :] = src_ref[layer, at(i * TILE), :]
            edge_ref[at(i * TILE + ahead + rows - skip), :] = src_ref[first, at(i * TILE), :]

    pl.when(with_even)(lambda: take(even_ref))
    pl.when(jnp.logical_not(with_even))(lambda: take(odd_ref))


def pick(bounds, sides, own, even, odd, before):
    _, rows, nz = own.shape
    skip = span(bounds, len(bounds) - 2, 1)[0] - (bounds[-2] - TILE)
    ahead = 0 if before is None else before.shape[0]
    return pl.pallas_call(
        functools.partial(pick_kernel, skip, ahead),
        out_shape=[
            jax.ShapeDtypeStruct(own.shape, own.dtype),
            jax.ShapeDtypeStruct((ahead + 2 * rows - skip, nz), own.dtype),
        ],
        in_specs=[SMEM] + [VMEM] * (4 if ahead else 3),
        out_specs=[VMEM, VMEM],
        cost_estimate=pl.CostEstimate(flops=0, bytes_accessed=8 * own.size, transcendentals=0),
        compiler_params=params(12),
        name="pick",
    )(sides, own, even, odd, *([before] if ahead else []))


def relax_rows(cells, mobility, outer, store, some, first, final, top, bottom, nz):
    def block(r, rows, top, bottom):
        lane = lax.broadcasted_iota(jnp.int32, (rows, LANES), 1)
        none = jnp.zeros((TILE, nz), jnp.float32)
        under = outer(r, rows) if some[0] == 0 else cells(some[0] - 1, r, rows)
        mid = cells(some[0], r, rows)
        for layer in some:
            over = cells(layer + 1, r, rows)
            above = none if top else cells(layer, r - TILE, TILE)
            below = none if bottom else cells(layer, r + rows, TILE)
            wide = jnp.concatenate([above, mid, below], axis=0)
            up, down = wide[TILE - 1 : TILE - 1 + rows], wide[TILE + 1 : TILE + 1 + rows]
            right = pltpu.roll(mid, nz - 1, 1)
            right = jnp.concatenate(
                [right[:, :-LANES], jnp.where(lane == LANES - 1, 0.0, right[:, -LANES:])], axis=1
            )
            left = pltpu.roll(mid, 1, 1)
            left = jnp.concatenate([jnp.where(lane == 0, 0.0, left[:, :LANES]), left[:, LANES:]], axis=1)
            beside = (over + under) + (down + up) + (right + left)
            rest = mid * (6.0 - 1.0 / EPS2 + (1.0 / EPS2) * (mid * mid))
            store(layer, r, rows, mid + (DT * EPS2 * mobility(layer, r, rows)) * (beside - rest))
            under, mid = mid, over

    for r in range(first, final, BLOCK):
        rows = min(BLOCK, final - r)
        block(r, rows, top and r == first, bottom and r + rows == final)


def outside():
    me, count = lax.axis_index("space"), lax.axis_size("space")
    return jnp.logical_or(me == 0, me == count - 1)


def margin(c, s):
    return 2 * TILE if c > 0 and 0 < s < STEPS else 0


def copy_ahead(ref):
    if "edge_before" not in ref:
        return 0
    rows = ref["edge_before"].shape[0]
    ref["edge"][:rows, :] = ref["edge_before"][...]
    return rows


def step_kernel(c, s, part, skip, bounds, layers, names, *refs):
    ref = dict(zip(names, refs))
    both = c == len(bounds) - 2
    last_step = s == STEPS
    ny, nz = ref["mob"].shape[1:]
    lo, hi = span(bounds, c, s)
    lead = margin(c, s)
    origin = 0 if s == 1 else span(bounds, c, s - 1)[0] - margin(c, s - 1)
    n_out = layers + STEPS - s
    some = {"edge": range(1), "inner": range(1, n_out), "outer": range(1)}.get(part, range(n_out))
    gives_edge = part in ("all", "edge") and not last_step
    gives_cells = part != "edge"
    no_outer = outside()

    def ghost_at(name, k, r, rows):
        return ref[name][k if c == 0 else layer_index(k, layers), at(r, rows), :]

    def cells(layer, r, rows):
        if s > 1:
            return ref["cells"][layer, at(r - origin, rows), :]
        if layer < layers:
            return ref["own"][layer_index(layer, layers), at(r, rows), :]
        return ghost_at("ghost", layer - layers, r, rows)

    def mobility(layer, r, rows):
        if layer < layers:
            return ref["mob"][layer_index(layer, layers), at(r, rows), :]
        return ghost_at("ghost_mob", layer - layers, r, rows)

    def outer(r, rows):
        return jnp.where(no_outer, 0.0, ref["beyond"][at(r - lo + skip, rows), :])

    edge_lo, edge_hi = span(bounds, c, s + 1) if not last_step else (0, 0)
    ahead = copy_ahead(ref) if gives_edge else 0
    out = ref["own_out"] if gives_cells else None

    def store(layer, r, rows, new):
        if gives_cells:
            out[layer - (some[0] if last_step else 0), at(r - lo + lead, rows), :] = new
        if layer > 0 or not gives_edge:
            return
        if r < edge_hi:
            kept = min(rows, edge_hi - r)
            ref["edge"][at(r - edge_lo + ahead, kept), :] = new[:kept]

    if c > 0 and not last_step:
        rows = ref["above"].shape[1]
        if gives_cells:
            for layer in range(n_out):
                out[layer, 0:lead, :] = ref["above"][layer, rows - lead : rows, :]
        if gives_edge:
            ref["edge"][ahead : ahead + TILE, :] = ref["above"][0, rows - TILE : rows, :]

    relax_rows(cells, mobility, outer, store, some, lo, hi, c == 0, both, nz)
    if not both:
        return

    start = bounds[-2] - TILE
    lo_other = other_first(bounds, s)
    sent, kept = hi - lo, edge_hi - edge_lo

    def other_cells(layer, r, rows):
        if s > 1:
            return ref["other"][layer, at(r - start, rows), :]
        src = ref["other"] if layer < layers else ref["other_ghost"]
        return src[layer_index(layer % layers, layers), at(r - start, rows), :]

    def other_outer(r, rows):
        return jnp.where(no_outer, 0.0, ref["beyond"][at(r - lo_other + sent + skip, rows), :])

    def other_store(layer, r, rows, new):
        if last_step:
            here = layer - some[0], at(r - lo, rows), slice(None)
            mine = out[here]
            out[here] = mine + ref["fractions"][0] * (new - mine)
            return
        if gives_cells:
            ref["other_out"][layer, at(r - start, rows), :] = new
        if layer == 0 and gives_edge:
            cut = max(0, other_first(bounds, s + 1) - r)
            ref["edge"][at(r + cut - other_first(bounds, s + 1) + kept + ahead, rows - cut), :] = new[cut:]

    relax_rows(other_cells, mobility, other_outer, other_store, some, lo_other, ny, not last_step, True, nz)
    if last_step:
        move(
            [(out.at[layer - some[0]], ref["out"].at[0, layer_index(layer, layers), lo:hi]) for layer in some],
            ref["sem"],
        )


def other_first(bounds, s):
    return bounds[-2] - (TILE if s < STEPS else 0)


def step(c, s, part, skip, bounds, layers, arrays, like, field, before):
    ny, nz = like.shape[1:]
    lo, hi = span(bounds, c, s)
    both = c == len(bounds) - 2
    n_out = layers + STEPS - s
    rows = ny - bounds[-2] + TILE
    own = (n_out, margin(c, s) + hi - lo, nz)
    last_both = both and s == STEPS
    in_specs = [SMEM if name == "fractions" else VMEM for name in arrays]
    shapes, scratch, aliases = {}, {}, {}
    if last_both:
        shapes["out"] = field.shape
        own = ({"inner": layers - 1, "outer": 1}.get(part, layers), *own[1:])
        scratch = {"own_out": pltpu.VMEM(own, like.dtype), "sem": pltpu.SemaphoreType.DMA((layers,))}
        if before is not None:
            aliases = {len(arrays): 0}
            arrays = {**arrays, "before": before}
            in_specs.append(ANY)
    else:
        if part != "edge":
            shapes["own_out"] = own
            if both:
                shapes["other_out"] = (n_out, rows, nz)
        if s < STEPS and part != "rest":
            edge_lo, edge_hi = span(bounds, c, s + 1)
            ahead = arrays["edge_before"].shape[0] if "edge_before" in arrays else 0
            shapes["edge"] = (ahead + edge_hi - edge_lo + (ny - other_first(bounds, s + 1) if both else 0), nz)
    cells = n_out * (hi - lo + (rows if both else 0)) * nz
    outs = pl.pallas_call(
        functools.partial(step_kernel, c, s, part, skip, bounds, layers, [*arrays, *shapes, *scratch]),
        out_shape=[jax.ShapeDtypeStruct(shape, like.dtype) for shape in shapes.values()],
        in_specs=in_specs,
        out_specs=[ANY] if last_both else [VMEM] * len(shapes),
        scratch_shapes=list(scratch.values()),
        input_output_aliases=aliases,
        cost_estimate=pl.CostEstimate(flops=20 * cells, bytes_accessed=4 * cells, transcendentals=0),
        compiler_params=params(12),
    )(*arrays.values())
    return dict(zip(shapes, outs))


def blend_kernel(spans, aliased, sides_ref, fractions_ref, *refs):
    n = len(spans)
    owns, evens, odds = refs[:n], refs[n : 2 * n], refs[2 * n : 3 * n]
    out_ref, bufs, sem = refs[3 * n + aliased], refs[3 * n + aliased + 1 : -1], refs[-1]
    layers = owns[0].shape[0]
    with_even = towards_even()(sides_ref[0])
    share = fractions_ref[0]
    copies = []
    for k, (lo, hi) in enumerate(spans):
        def mix(other_ref, own_ref=owns[k], buf=bufs[k], rows=hi - lo):
            @pl.loop(0, rows // TILE)
            def _(i):
                for layer in range(layers):
                    mine = own_ref[layer, at(i * TILE), :]
                    buf[layer, at(i * TILE), :] = mine + share * (other_ref[layer, at(i * TILE), :] - mine)

        pl.when(with_even)(functools.partial(mix, evens[k]))
        pl.when(jnp.logical_not(with_even))(functools.partial(mix, odds[k]))
        for layer in range(layers):
            copy = pltpu.make_async_copy(
                bufs[k].at[layer], out_ref.at[0, layer_index(layer, layers), lo:hi], sem.at[k, layer]
            )
            copy.start()
            copies.append(copy)
    for copy in copies:
        copy.wait()


def blend(chunks, bounds, sides, fractions, val, out, like):
    spans = [span(bounds, c, STEPS) for c in chunks]
    owns = [val["K", c, STEPS] for c in chunks]
    layers = owns[0].shape[0]
    operands = [sides, fractions, *owns, *(val["Z", c, name] for name in ("even", "odd") for c in chunks)]
    size = sum(own.size for own in owns)
    return pl.pallas_call(
        functools.partial(blend_kernel, spans, out is not None),
        out_shape=jax.ShapeDtypeStruct(like.shape, like.dtype),
        in_specs=[SMEM, SMEM] + [VMEM] * (3 * len(chunks)) + ([] if out is None else [HBM]),
        out_specs=HBM,
        input_output_aliases={} if out is None else {len(operands): 0},
        scratch_shapes=[pltpu.VMEM(own.shape, own.dtype) for own in owns]
        + [pltpu.SemaphoreType.DMA((len(chunks), layers))],
        cost_estimate=pl.CostEstimate(flops=3 * size, bytes_accessed=12 * size, transcendentals=0),
        compiler_params=params(12),
    )(*operands, *([] if out is None else [out]))


def items():
    return " ".join(ORDER).split()


def chunk_of(name):
    return len(SHARES) if name == "A" else int(name)


def swaps():
    ahead = {}
    for item in items():
        members = [(chunk_of(m[0]), int(m[1])) for m in item[1:].split("_")] if item[0] == "O" else []
        ahead.update(zip(members[1:], members))
    return ahead


def local(field, mobility, fractions, sides):
    layers, ny = field.shape[1:3]
    bounds = cuts(ny)
    last = len(bounds) - 2
    ahead = swaps()
    val = {}
    out = None

    def before(c, s):
        return val["edge", ahead[c, s]] if (c, s) in ahead else None

    for item in items():
        kind = item[0]
        if kind == "E":
            val["edge", (0, 1)] = first_edge(field, bounds)
        elif kind == "G":
            val["near"] = near_ghosts(field, bounds)
        elif kind == "L":
            val["near_mob"], val["K", last, STEPS], *edges = later_edges(field, mobility, bounds)
            for i, edge in zip((1, *range(TOGETHER + 1, last)), edges):
                val["edge", (i, 1)] = edge
        elif kind == "C":
            sources = {"n": "near", "o": "near_mob", "N": "N", "f": field[0], "m": mobility}
            source = sources[item[1]]
            val["C", item[1]] = swap(val[source] if isinstance(source, str) else source, 0)
        elif kind == "N":
            val["N"], val["edge", (last, 1)] = pick(
                bounds,
                sides,
                val["K", last, STEPS],
                val["Z", last, "even"],
                val["Z", last, "odd"],
                before(last, 1),
            )
        elif kind == "O":
            members = [(chunk_of(m[0]), int(m[1])) for m in item[1:].split("_")]
            got = swap(val["edge", members[-1]], 1)
            skip = 0
            for c, s in members:
                val["O", c, s] = got, skip
                lo, hi = raw_group(bounds, c) if s == 1 else span(bounds, c, s)
                if (c, s) == (1, 1):
                    for i in range(2, TOGETHER + 1):
                        val["O", i, 1] = got, skip + span(bounds, i, 1)[0] - lo
                skip += hi - lo + (ny - other_first(bounds, s) if c == last else 0)
        elif kind in "KJI":
            c, s = chunk_of(item[1]), int(item[2])
            split = c == last
            part = "all"
            if split:
                part = {"J": "edge", "I": "inner"}.get(kind, "rest" if s < STEPS else "outer")
            beyond, skip = val["O", c, s] if part != "inner" else (None, 0)
            arrays = {"mob": mobility}
            if beyond is not None:
                arrays["beyond"] = beyond
            arrays["ghost_mob"] = val["C", "m" if c > 0 else "o"]
            if s == 1:
                arrays["ghost"] = val["C", "f" if c > 0 else "n"]
                arrays["own"] = field[0]
            else:
                arrays["cells"] = val["K", c, s - 1]
            if c > 0 and s < STEPS:
                arrays["above"] = val["K", c - 1, s]
            if c == last:
                arrays["other"] = val["N"] if s == 1 else val["other", s - 1]
                if s == 1:
                    arrays["other_ghost"] = val["C", "N"]
                if s == STEPS:
                    arrays["fractions"] = fractions
            if before(c, s + 1) is not None and part in ("all", "edge"):
                arrays["edge_before"] = before(c, s + 1)
            got = step(c, s, part, skip, bounds, layers, arrays, mobility, field, out)
            out = got.get("out", out)
            for name, key in (("own_out", ("K", c, s)), ("other_out", ("other", s)), ("edge", ("edge", (c, s + 1)))):
                if name in got:
                    val[key] = got[name]
        elif kind == "Z":
            c = chunk_of(item[1])
            for name, odd in (("even", 0), ("odd", 1)):
                val["Z", c, name] = swap_images(val["K", c, STEPS], odd)
        elif kind == "B":
            out = blend(BLENDS[int(item[1])], bounds, sides, fractions, val, out, field)
    return out


def solution(mesh):
    return jax.shard_map(
        local,
        mesh=mesh,
        in_specs=(P("image", "space", None, None), P("space", None, None), P("image"), P("image")),
        out_specs=P("image", "space", None, None),
        check_vma=False,
    )
```
